32 devices in a mesh: seq: 8 (over z, core), tp: 4 (over y, x).
Axes of the slice: x: 2, y: 2, z: 4, core: 2. Of those that a mesh axis runs over, the one named last changes fastest.
Arguments:
- latents: bfloat16 [8, 4096, 512], P(None, ('seq', 'tp')), may hold values from -6 to 6
- rotary_rows: bfloat16 [8, 4096, 64], P(None, ('seq', 'tp')), may hold values from -6 to 6
- latent_gain: float32 [512], replicated, may hold values from 0.25 to 1.75
- key_up: bfloat16 [512, 16, 128], P(None, 'tp'), may hold values from -0.25 to 0.25
- value_up: bfloat16 [512, 16, 128], P(None, 'tp'), may hold values from -0.25 to 0.25
Outputs:
- decode_keys: bfloat16 [8, 16, 192, 4096], P('seq', 'tp')
- decode_values: bfloat16 [8, 4096, 16, 128], P('seq', None, 'tp')
The draws below stay inside these ranges and needn't reach their ends.
All inputs are finite; a program needn't handle non-finite values.
Results may differ from the reference program's by a relative error of at most 0.0049.
Values may be sent and summed in bfloat16 or wider, within the bound.
A program may use at most 64 MiB of HBM per device.

```python
import jax
import jax.numpy as jnp
from jax import lax

BATCH = 8
LENGTH = 4096
HEADS = 16
LATENT = 512
KEY_PART = 128
ROTARY = 64
VALUE_SIZE = 128


def levels(own_key, dims, shards, smallest, high):
    def one(dim, blocks):
        steps = jax.random.uniform(jax.random.fold_in(jax.random.fold_in(own_key, 6), dim), (blocks,), jnp.float32, smallest / len(shards), high / len(shards))
        return jnp.repeat(jnp.exp(steps), dims[dim] // blocks).reshape((-1,) + (1,) * (len(dims) - dim - 1))

    loudness = one(*shards[0])
    for cut in shards[1:]:
        loudness = loudness * one(*cut)
    return loudness


def bell_draw(rng, dims, width, limit, split=(), held_as=jnp.bfloat16):
    factor_of = levels(rng, dims, split, -0.22, 0.18) if split else 1.0
    array = jax.random.normal(rng, dims, jnp.float32) * width * factor_of
    return jnp.minimum(jnp.maximum(array, -limit), limit).astype(held_as)


def setup_inputs(seed: int = 0) -> dict:
    arg_keys = jax.random.split(jax.random.key(seed), 6)
    latents = bell_draw(arg_keys[0], (BATCH, LENGTH, LATENT), 1.0, 6.0, ((1, 32),))
    rotary_rows = bell_draw(arg_keys[1], (BATCH, LENGTH, ROTARY), 1.0, 6.0, ((1, 32),))
    latent_gain = jnp.clip(1.0 + 0.15 * jax.random.normal(arg_keys[2], (LATENT,), jnp.float32), 0.25, 1.75)
    key_up = bell_draw(arg_keys[3], (LATENT, HEADS, KEY_PART), LATENT ** -0.5, 0.25, ((1, 4),))
    value_up = bell_draw(arg_keys[4], (LATENT, HEADS, VALUE_SIZE), LATENT ** -0.5, 0.25, ((1, 4),))
    return dict(latents=latents, rotary_rows=rotary_rows, latent_gain=latent_gain, key_up=key_up, value_up=value_up)


def root_norm(vectors, row_gain):
    return vectors * lax.rsqrt(lax.optimization_barrier(jnp.mean(vectors * vectors, axis=-1, keepdims=True)) + 1e-06) * row_gain

def reference(latents, rotary_rows, latent_gain, key_up, value_up):
    rows_ready = root_norm(latents.astype(jnp.float32), latent_gain).astype(jnp.bfloat16)
    rows_ready = lax.optimization_barrier(rows_ready)

    def expand_one(one):
        rows_one, rotary_one = one
        wide_keys = jnp.einsum('tr,rhk->thk', rows_one.astype(jnp.float32), key_up.astype(jnp.float32)).astype(jnp.bfloat16)
        shared = jnp.broadcast_to(rotary_one[:, None], (LENGTH, HEADS, ROTARY))
        wide_values = jnp.einsum('tr,rhk->thk', rows_one.astype(jnp.float32), value_up.astype(jnp.float32)).astype(jnp.bfloat16)
        return (jnp.concatenate([wide_keys, shared], axis=-1), wide_values)
    decode_keys, decode_values = lax.map(expand_one, (rows_ready, rotary_rows))
    decode_keys = jnp.transpose(decode_keys, (0, 2, 3, 1))
    return (decode_keys, decode_values)
```

```python
import jax
import jax.numpy as jnp
from jax import lax
from jax.sharding import PartitionSpec as P


def expand_rows(rows, rotary, key_up, value_up):
    wide_keys = jnp.einsum(
        "rhk,brt->bhkt", key_up, rows, preferred_element_type=jnp.float32
    ).astype(jnp.bfloat16)
    shared = jnp.broadcast_to(
        rotary[:, None], wide_keys.shape[:2] + rotary.shape[1:]
    )
    wide_values = jnp.einsum(
        "brt,rhk->bthk", rows, value_up, preferred_element_type=jnp.float32
    ).astype(jnp.bfloat16)
    return (jnp.concatenate([wide_keys, shared], axis=2), wide_values)


def root_norm(vectors, row_gain):
    return (
        vectors * lax.rsqrt(jnp.mean(vectors * vectors, axis=-1, keepdims=True) + 1e-06) * row_gain
    )


def shards(latents, rotary_rows, latent_gain, key_up, value_up):
    rows_ready = root_norm(latents.astype(jnp.float32), latent_gain).astype(jnp.bfloat16)
    latent = rows_ready.shape[2]
    packed = jnp.concatenate(
        [jnp.swapaxes(rows_ready, 1, 2), jnp.swapaxes(rotary_rows, 1, 2)], axis=1
    )
    seq_size = lax.axis_size("seq")
    moved = lax.all_to_all(packed, "seq", split_axis=0, concat_axis=0, tiled=True)
    joined = lax.all_gather(moved, "tp", axis=0, tiled=False)
    tp_size = joined.shape[0]
    whole = joined.reshape(tp_size, seq_size, -1, joined.shape[2], joined.shape[3])
    whole = jnp.transpose(whole, (2, 3, 1, 0, 4))
    whole = whole.reshape(whole.shape[0], whole.shape[1], -1)
    return expand_rows(whole[:, :latent], whole[:, latent:], key_up, value_up)


def solution(mesh):
    return jax.shard_map(
        shards,
        mesh=mesh,
        in_specs=(
            P(None, ("seq", "tp"), None),
            P(None, ("seq", "tp"), None),
            P(),
            P(None, "tp", None),
            P(None, "tp", None),
        ),
        out_specs=(P("seq", "tp", None, None), P("seq", None, "tp", None)),
        check_vma=False,
    )
```
